32 devices in a mesh: frame: 4 (over y, x), seq: 8 (over z, core).
Axes of the slice: x: 2, y: 2, z: 4, core: 2. Of those that a mesh axis runs over, the one named last changes fastest.
Arguments:
- latent: bfloat16 [1, 4, 512, 1152], P(None, 'frame', 'seq'), may hold values from -6 to 6
- attention_weights: bfloat16 [2, 4, 1152, 1152], P(None, None, 'frame'), may hold values from -3 to 3
- modulation: float32 [16, 2, 3, 1152], replicated, may hold values from -3 to 3
- step_factors: float32 [16, 2], replicated, may hold values from 0.3 to 0.9
- timesteps: int32 [4], replicated, may hold values from 0 to 15
- plan: int32 [4, 2], replicated, may hold values from 0 to 2, as said below
Outputs:
- denoised: bfloat16 [1, 4, 512, 1152], P(None, 'frame', 'seq')
The draws below stay inside these ranges and needn't reach their ends.
Inputs may be any that keep to these rules, and one draw needn't show every extreme that they name: plan[s, j] is at most min(s, 2): row 0 is all zeros and row 1 holds only 0 and 1.
All inputs are finite; a program needn't handle non-finite values.
Results may differ from the reference program's by a relative error of at most 0.013.
Values may be sent and summed in bfloat16 or wider, within the bound.
No kernel may reach another device: no remote copies, remote signals or barrier semaphores. Data moves between devices by JAX's collectives and lax.ppermute only.
A program may use at most 128 MiB of HBM per device.

```python
import math
import jax
import jax.numpy as jnp
from jax import lax

D = 1152
HEADS = 16
BATCH = 1
STEPS = 4
TABLE = 16
FRAMES = 4
FRAME_TOKENS = 512


def draw_attention_weights(key, part):
    first_key = jax.random.fold_in(jax.random.fold_in(key, 11), 0)
    weights_base = jax.random.normal(first_key, (2, 4, D, D), jnp.float32) * D ** (-0.5)
    return jnp.clip(weights_base, -3.0, 3.0).astype(jnp.bfloat16)


def draw_plan(key, part):
    raw_codes = jax.random.randint(jax.random.fold_in(key, 23), (STEPS, 2), 0, 3)
    ceiling = jnp.minimum(jnp.arange(STEPS, dtype=jnp.int32), 2)[:, None]
    return jnp.minimum(raw_codes, ceiling).astype(jnp.int32)


def set_ends(array, stream_key, low, largest):
    longest = array.shape.index(max(array.shape))
    spots = []
    for shift in (0, 1):
        where = [jax.random.randint(jax.random.fold_in(stream_key, axis), (), 0, length) for axis, length in enumerate(array.shape)]
        where[longest] = (where[longest] + shift) % array.shape[longest]
        spots.append(tuple(where))
    return array.at[spots[0]].set(low).at[spots[1]].set(largest)


def block_scale(own_key, extent, cuts, smallest, top_value):
    loudness, own = 1.0, jax.random.fold_in(own_key, 6)
    for dim, parts in cuts:
        heights = jnp.exp(jax.random.uniform(jax.random.fold_in(own, dim), (parts,), jnp.float32, smallest / len(cuts), top_value / len(cuts)))
        loudness = loudness * jnp.repeat(heights, extent[dim] // parts).reshape([-1 if axis == dim else 1 for axis in range(len(extent))])
    return loudness


def scatter_about(stream_key, extent, scale, reach, cuts=(), kind=jnp.bfloat16):
    entries = scale * jax.random.normal(stream_key, extent, jnp.float32)
    if cuts:
        entries = entries * block_scale(stream_key, extent, cuts, -0.22, 0.18)
    return jnp.clip(entries, -reach, reach).astype(kind)


def setup_inputs(seed: int = 0) -> dict:
    streams_of = jax.random.split(jax.random.key(seed), 7)
    return {
        "latent": scatter_about(streams_of[0], (BATCH, FRAMES, FRAME_TOKENS, D), 1.0, 6.0, ((1, 4), (2, 8))),
        "attention_weights": draw_attention_weights(jax.random.fold_in(streams_of[6], 71), 0),
        "modulation": scatter_about(streams_of[2], (TABLE, 2, 3, D), 0.5, 3.0, (), jnp.float32),
        "step_factors": jnp.clip(jax.random.uniform(streams_of[3], (TABLE, 2), jnp.float32, 0.3, 0.9), 0.3, 0.9),
        "timesteps": set_ends(jax.random.randint(streams_of[4], (STEPS,), 0, TABLE), jax.random.fold_in(streams_of[4], 1), 0, TABLE - 1).astype(jnp.int32),
        "plan": draw_plan(jax.random.fold_in(streams_of[6], 71), 0),
    }


EPSILON = 1e-06

def norm_modulate(hidden_state, offset, stretch):
    row_mean = lax.optimization_barrier(jnp.mean(hidden_state, axis=-1, keepdims=True))
    centred = hidden_state - row_mean
    row_var = lax.optimization_barrier(jnp.mean(centred * centred, axis=-1, keepdims=True))
    return (centred * lax.rsqrt(row_var + EPSILON) * (1.0 + stretch) + offset).astype(jnp.bfloat16)

def attend(queries, key_rows, value_rows):
    head_size = queries.shape[-1]
    scores = jnp.einsum('...qhc,...khc->...hqk', queries.astype(jnp.float32), key_rows.astype(jnp.float32)) / math.sqrt(head_size)
    row_max = lax.optimization_barrier(jnp.max(scores, axis=-1, keepdims=True))
    probs = jnp.exp(scores - row_max)
    row_sum = lax.optimization_barrier(jnp.sum(probs, axis=-1))
    rounded = lax.optimization_barrier(probs.astype(jnp.bfloat16))
    attended = jnp.einsum('...hqk,...khc->...qhc', rounded.astype(jnp.float32), value_rows.astype(jnp.float32))
    return (attended / jnp.swapaxes(row_sum, -1, -2)[..., None]).astype(jnp.bfloat16)

def branch(hidden_state, weight_set, step_mods, block_index):
    batch_count, frame_count, token_count, width = hidden_state.shape
    head_size = width // HEADS
    normed = norm_modulate(hidden_state, step_mods[0], step_mods[1])
    flat_rows = normed.reshape(-1, width)
    split_shape = (batch_count, frame_count, token_count, HEADS, head_size)
    queries = jnp.dot(flat_rows, weight_set[0], preferred_element_type=jnp.float32).astype(jnp.bfloat16).reshape(split_shape)
    key_rows = jnp.dot(flat_rows, weight_set[1], preferred_element_type=jnp.float32).astype(jnp.bfloat16).reshape(split_shape)
    value_rows = jnp.dot(flat_rows, weight_set[2], preferred_element_type=jnp.float32).astype(jnp.bfloat16).reshape(split_shape)
    if block_index == 0:
        seq_shape = (batch_count * frame_count, token_count, HEADS, head_size)
        attended = lax.map(lambda triple: attend(triple[0], triple[1], triple[2]), (queries.reshape(seq_shape), key_rows.reshape(seq_shape), value_rows.reshape(seq_shape)))
    else:
        attended = jnp.swapaxes(attend(jnp.swapaxes(queries, 1, 2), jnp.swapaxes(key_rows, 1, 2), jnp.swapaxes(value_rows, 1, 2)), 1, 2)
    mixed = jnp.dot(attended.reshape(-1, width), weight_set[3], preferred_element_type=jnp.float32)
    return (mixed.reshape(hidden_state.shape) * step_mods[2]).astype(jnp.bfloat16)

def reference(latent, attention_weights, modulation, step_factors, timesteps, plan):
    current = latent
    cache_slots = jnp.zeros((2, 2) + latent.shape, jnp.bfloat16)
    for step_index in range(STEPS):
        moment = timesteps[step_index]
        step_mods = modulation[moment]
        factors = step_factors[moment]
        hidden_state = current.astype(jnp.float32)
        fresh_updates = []
        for block_index in range(2):
            reuse_code = plan[step_index, block_index]
            stored = jnp.where(reuse_code == 2, cache_slots[1, block_index], cache_slots[0, block_index])
            computed = branch(hidden_state, attention_weights[block_index], step_mods[block_index], block_index)
            update = jnp.where(reuse_code == 0, computed, stored)
            hidden_state = hidden_state + update.astype(jnp.float32)
            fresh_updates.append(update)
        current = (factors[0] * current.astype(jnp.float32) + factors[1] * hidden_state).astype(jnp.bfloat16)
        cache_slots = jnp.stack([jnp.stack(fresh_updates), cache_slots[0]])
    return current
```

```python
import functools
import math

import jax
import jax.numpy as jnp
from jax import lax
from jax.experimental import pallas as pl
from jax.experimental.pallas import tpu as pltpu
from jax.sharding import PartitionSpec as P

HEADS = 16
CORES = 2
LANES = 128
EPSILON = 1e-06
MASKED = -1e30
BOTH = ("frame", "seq")


def kernel_params(mib):
    return pltpu.CompilerParams(vmem_limit_bytes=mib << 20)


def run(kernel, outs, *args, mib=16, flops=0):
    moved = sum(a.size * a.dtype.itemsize for a in args)
    moved += sum(math.prod(o.shape) * o.dtype.itemsize for o in outs)
    return pl.pallas_call(
        kernel,
        out_shape=outs,
        in_specs=[pl.BlockSpec(memory_space=pltpu.VMEM)] * len(args),
        out_specs=[pl.BlockSpec(memory_space=pltpu.VMEM)] * len(outs),
        compiler_params=kernel_params(mib),
        cost_estimate=pl.CostEstimate(flops=flops, bytes_accessed=moved, transcendentals=0),
    )(*args)


def bf16(*shape):
    return jax.ShapeDtypeStruct(shape, jnp.bfloat16)


def norm_kernel(row, hidden_ref, mods_ref, out_ref):
    hidden = hidden_ref[...]
    width = hidden.shape[-1]
    mean = jnp.sum(hidden, axis=-1, keepdims=True) / width
    centred = hidden - mean
    var = jnp.sum(centred * centred, axis=-1, keepdims=True) / width
    stretch = 1.0 + mods_ref[row + 1 : row + 2, :]
    offset = mods_ref[row : row + 1, :]
    out_ref[...] = (centred * lax.rsqrt(var + EPSILON) * stretch + offset).astype(jnp.bfloat16)


def project(x, weights_ref, member, heads, head_size):
    y = jnp.dot(x, weights_ref[member], preferred_element_type=jnp.float32)
    rows = y.shape[0]
    blank = jnp.zeros((rows, LANES - head_size), jnp.float32)
    pieces = []
    for h in range(heads):
        pieces.append(y[:, h * head_size : (h + 1) * head_size])
        pieces.append(blank)
    return [
        jnp.concatenate(pieces[2 * h : 2 * h + 2], axis=-1).astype(jnp.bfloat16)
        for h in range(heads)
    ]


def qkv_kernel(heads, head_size, *refs):
    *x_refs, weights_ref, q_ref, kv_ref = refs
    x = jnp.concatenate([r[...] for r in x_refs], axis=0)
    for member in range(3):
        parts = project(x, weights_ref, member, heads, head_size)
        for h, part in enumerate(parts):
            if member == 0:
                q_ref[:, h * LANES : (h + 1) * LANES] = part
            else:
                at = (h * 2 + member - 1) * LANES
                kv_ref[:, at : at + LANES] = part


def attend(q, k, v, head_size, mask):
    scores = lax.dot_general(
        q, k, (((1,), (1,)), ((), ())), preferred_element_type=jnp.float32
    ) / math.sqrt(head_size)
    if mask is not None:
        scores = jnp.where(mask, scores, MASKED)
    probs = jnp.exp(scores - jnp.max(scores, axis=-1, keepdims=True))
    total = jnp.sum(probs, axis=-1, keepdims=True)
    mixed = jnp.dot(probs.astype(jnp.bfloat16), v, preferred_element_type=jnp.float32)
    return (mixed / total).astype(jnp.bfloat16)


def put_out(attended, out_weights_ref, y_refs):
    joined = jnp.concatenate(attended, axis=-1)
    y = jnp.dot(joined, out_weights_ref[...], preferred_element_type=jnp.float32)
    rows = y.shape[0] // len(y_refs)
    for k, ref in enumerate(y_refs):
        ref[...] = y[k * rows : (k + 1) * rows].astype(jnp.bfloat16)


def spatial_kernel(heads, head_size, q_ref, own_ref, other_ref, out_weights_ref, *y_refs):
    attended = []
    for h in range(heads):
        at = 2 * h * LANES
        k = jnp.concatenate([r[:, at : at + LANES] for r in (own_ref, other_ref)], axis=0)
        v = jnp.concatenate(
            [r[:, at + LANES : at + 2 * LANES] for r in (own_ref, other_ref)], axis=0
        )
        q = q_ref[:, h * LANES : (h + 1) * LANES]
        attended.append(attend(q, k, v, head_size, None))
    put_out(attended, out_weights_ref, y_refs)


def temporal_kernel(heads, head_size, groups, *refs):
    x_refs, (weights_ref, out_weights_ref), y_refs = (
        refs[:groups],
        refs[groups : groups + 2],
        refs[groups + 2 :],
    )
    x = jnp.concatenate([r[...] for r in x_refs], axis=0)
    rows, tokens = x.shape[0], x_refs[0].shape[0]
    q, k, v = (project(x, weights_ref, m, heads, head_size) for m in range(3))
    row = lax.broadcasted_iota(jnp.int32, (rows, rows), 0)
    column = lax.broadcasted_iota(jnp.int32, (rows, rows), 1)
    mask = lax.rem(row, tokens) == lax.rem(column, tokens)
    attended = [attend(q[h], k[h], v[h], head_size, mask) for h in range(heads)]
    put_out(attended, out_weights_ref, y_refs)


def sum_kernel(row, mods_ref, *refs):
    *y_refs, out_ref = refs
    total = sum(r[...].astype(jnp.float32) for r in y_refs)
    out_ref[...] = (total * mods_ref[row : row + 1, :]).astype(jnp.bfloat16)


def shift(x, axis, size, step, by):
    return lax.ppermute(x, axis, [(i, (i + by * step) % size) for i in range(size)])


def swap_cores(x, size):
    return lax.ppermute(x, "seq", [(i, i ^ 1) for i in range(size)])


def pad_heads(out_weights, heads):
    rows, width = out_weights.shape
    split = out_weights.reshape(heads, rows // heads, width)
    padded = jnp.pad(split, ((0, 0), (0, LANES - rows // heads), (0, 0)))
    return padded.reshape(heads * LANES, width)


def whole_rows(half, core, seq):
    other = swap_cores(half, seq)
    members, shards, rows, columns = half.shape
    first = jnp.where(core == 0, half, other)
    second = jnp.where(core == 0, other, half)
    both = jnp.stack([first, second], axis=2)
    return both.reshape(members, shards * CORES * rows, columns)


def body(latent, attention_weights, modulation, step_factors, timesteps, plan):
    frames, seq = lax.axis_size("frame"), lax.axis_size("seq")
    chips = seq // CORES
    frame, place = lax.axis_index("frame"), lax.axis_index("seq")
    chip, core = place // CORES, place % CORES
    _, _, tokens, width = latent.shape
    head_size = width // HEADS
    shard = attention_weights.shape[2]
    half = shard // CORES
    groups = (chips, frames)
    heads = (HEADS // chips, HEADS // frames)
    columns = tuple(n * head_size for n in heads)
    steps = timesteps.shape[0]

    def chip_shift(x, by):
        return shift(x, "seq", seq, CORES, by)

    def frame_shift(x, by):
        return shift(x, "frame", frames, 1, by)

    moves = (chip_shift, frame_shift)

    mine = lax.dynamic_slice_in_dim(attention_weights[:, :3], core * half, half, 2)

    def gather_rows(block, choose):
        gathered = jnp.zeros((3, frames, half, columns[block]), jnp.bfloat16)
        for k in range(frames):
            piece = lax.dynamic_slice_in_dim(
                mine[block], choose(k) * columns[block], columns[block], 2
            )
            piece = frame_shift(piece, k) if k else piece
            gathered = lax.dynamic_update_index_in_dim(
                gathered, piece, (frame - k) % frames, 1
            )
        return whole_rows(gathered, core, seq)

    in_weights = (
        gather_rows(0, lambda k: chip),
        gather_rows(1, lambda k: (frame + k) % frames),
    )

    ratio = frames // chips
    pieces = jnp.zeros((ratio, shard, width), jnp.bfloat16)
    for p in range(ratio):
        pairs = []
        for f in range(frames):
            for z in range(chips):
                for c in range(CORES):
                    source = (ratio * z + (p + f) % ratio) * seq + (f // ratio) * CORES + c
                    pairs.append((source, f * seq + z * CORES + c))
        piece = lax.ppermute(attention_weights[0, 3], BOTH, pairs)
        pieces = lax.dynamic_update_index_in_dim(pieces, piece, (p + frame) % ratio, 0)
    out_weights = (
        pad_heads(pieces.reshape(ratio * shard, width), heads[0]),
        pad_heads(attention_weights[1, 3], heads[1]),
    )

    mods = jnp.take(modulation, timesteps, axis=0).reshape(steps * 6, width)
    factors = jnp.take(step_factors, timesteps, axis=0)

    def branch(hidden, step, block):
        row = 6 * step + 3 * block
        n, move = groups[block], moves[block]
        (normed,) = run(functools.partial(norm_kernel, row), [bf16(tokens, width)], hidden, mods)
        gathered = [normed] + [move(normed, k) for k in range(1, n)]
        outs = [bf16(tokens, width)] * n
        rows = n * tokens
        inner = heads[block] * LANES
        if block == 0:
            q, kv = run(
                functools.partial(qkv_kernel, heads[0], head_size),
                [bf16(rows, inner), bf16(rows, 2 * inner)],
                *gathered,
                in_weights[0],
                flops=2 * rows * width * 3 * inner,
            )
            other = swap_cores(kv, seq)
            results = run(
                functools.partial(spatial_kernel, heads[0], head_size),
                outs,
                q,
                kv,
                other,
                out_weights[0],
                flops=2 * rows * inner * (4 * rows + width),
            )
        else:
            results = run(
                functools.partial(temporal_kernel, heads[1], head_size, n),
                outs,
                *gathered,
                in_weights[1],
                out_weights[1],
                flops=2 * rows * inner * (3 * width + 2 * rows + width),
            )
        returned = [results[0]] + [move(results[k], -k) for k in range(1, n)]
        (update,) = run(
            functools.partial(sum_kernel, row + 2), [bf16(tokens, width)], mods, *returned
        )
        return update

    current = latent.reshape(tokens, width)
    stored = [[None, None], [None, None]]
    for step in range(steps):
        hidden = current.astype(jnp.float32)
        fresh = []
        for block in range(2):
            if step == 0:
                update = branch(hidden, step, block)
            else:
                code = plan[step, block]
                kept = stored[0][block]
                if step > 1:
                    kept = jnp.where(code == 2, stored[1][block], kept)
                update = lax.cond(
                    code == 0,
                    lambda h, kept, step=step, block=block: branch(h, step, block),
                    lambda h, kept: kept,
                    hidden,
                    kept,
                )
            hidden = hidden + update.astype(jnp.float32)
            fresh.append(update)
        current = (
            factors[step, 0] * current.astype(jnp.float32) + factors[step, 1] * hidden
        ).astype(jnp.bfloat16)
        stored = [fresh, stored[0]]
    return current.reshape(latent.shape)


def solution(mesh):
    placed = (P(None, "frame", "seq", None), P(None, None, "frame", None), P(), P(), P(), P())
    return jax.shard_map(
        body, mesh=mesh, in_specs=placed, out_specs=P(None, "frame", "seq", None), check_vma=False
    )
```
